32 devices in a mesh: ctx: 2 (over y), state: 4 (over z), expert: 4 (over x, core).
Axes of the slice: x: 2, y: 2, z: 4, core: 2. Of those that a mesh axis runs over, the one named last changes fastest.
Arguments:
- tokens: bfloat16 [256, 8192], P('ctx', ('state', 'expert')), may hold values from -6 to 6
- ssm_input: bfloat16 [256, 16384], P('ctx', ('state', 'expert')), may hold values from -6 to 6
- in_b: bfloat16 [256, 128], P('ctx'), may hold values from -1.75 to 1.75
- in_c: bfloat16 [256, 128], P('ctx'), may hold values from -1.75 to 1.75
- decay_log: float32 [256, 64], P('ctx', ('state', 'expert')), may hold values from -0.6 to 0, as said below
- skip_gain: float32 [64], P(('state', 'expert')), may hold values from 0.1 to 1.9
- out_proj: bfloat16 [16384, 8192], P(('state', 'expert'), 'ctx'), may hold values from -0.046875 to 0.046875
- norm_gain: float32 [8192], P(('state', 'expert')), may hold values from 0.1 to 1.9
- routes: int32 [256, 2], P('ctx'), may hold values from 0 to 3, all different within a row; in each aligned block of 128 rows (0 to 127, 128 to 255, ...) at most 80 rows name the same one
- route_gate: float32 [256, 2], P('ctx'), may hold values from 0.2 to 1
- w_gate: bfloat16 [4, 8192, 12288], P('expert', None, ('ctx', 'state')), may hold values from -0.0625 to 0.0625
- w_up: bfloat16 [4, 8192, 12288], P('expert', None, ('ctx', 'state')), may hold values from -0.0625 to 0.0625
- w_down: bfloat16 [4, 12288, 8192], P('expert', ('ctx', 'state')), may hold values from -0.0546875 to 0.0546875
Outputs:
- block_out: bfloat16 [256, 8192], P('ctx', ('state', 'expert'))
The draws below stay inside these ranges and needn't reach their ends.
Inputs may be any that keep to these rules, and one draw needn't show every extreme that they name: decay_log is never positive. `routes`: in each block of 128 rows (the rows of one index of ctx) no expert is named by more than 80 rows, and in some block one expert is named by exactly 80 rows.
All inputs are finite; a program needn't handle non-finite values.
Results may differ from the reference program's by a relative error of at most 0.017.
Values may be sent and summed in bfloat16 or wider, within the bound.
A program may use at most 192 MiB of HBM per device.

```python
import math
import jax
import jax.numpy as jnp
import numpy as np
from jax import lax

D = 8192
HEADS = 64
HEAD_DIM = 256
NSTATE = 128
D_INNER = 16384
FF = 12288
EXPERTS = 4
TOK_CTX = 128
TOKENS = 256
MOST = 80
N_CTX = 2
N_STATE = 4
N_EXPERT = 4


def draw_decay_log(key, part):
    keys = jax.random.split(jax.random.fold_in(key, 17), 6)
    share = 0.5
    patient = jax.random.uniform(keys[0], (HEADS,)) < share
    patient_rate = jax.random.uniform(keys[1], (HEADS,), minval=0.05, maxval=0.6) / TOKENS
    hasty_rate = jax.random.uniform(keys[2], (HEADS,), minval=1.0 / 50.0, maxval=1.0 / 30.0)
    rate_head = jnp.where(patient, patient_rate, hasty_rate)
    rough = jax.random.uniform(keys[3], (TOKENS, HEADS), minval=0.5, maxval=1.5)
    spots = jax.random.randint(keys[4], (2,), 0, TOKENS)
    marked = jnp.any(jnp.arange(TOKENS)[:, None] == spots[None, :], axis=1)
    losses = jax.random.uniform(keys[5], (TOKENS, HEADS), minval=0.22, maxval=0.51)
    result = -(rate_head[None, :] * rough + jnp.where(marked[:, None], losses, 0.0))
    return result.astype(jnp.float32)


def levels(own_key, shape, cuts, low, top_value):
    def one(dim, shards_of):
        heights = jax.random.uniform(jax.random.fold_in(jax.random.fold_in(own_key, 6), dim), (shards_of,), jnp.float32, low / len(cuts), top_value / len(cuts))
        return jnp.repeat(jnp.exp(heights), shape[dim] // shards_of).reshape((-1,) + (1,) * (len(shape) - dim - 1))

    factor_of = one(*cuts[0])
    for cut in cuts[1:]:
        factor_of = factor_of * one(*cut)
    return factor_of


def assign_block(rng, own, number, rows, amount, top, most, lean):
    ranking = jax.random.permutation(rng, amount)
    crowded, common = shares(amount, rows * top, most, lean, True), shares(amount, rows * top, most, lean, False)
    places = jnp.arange(amount)

    def named(lengths, rotation):
        used = int((lengths > 0).sum())
        fixed = max(1, used // 4)
        shifted = fixed + (places - fixed + rotation * (used - fixed)) % max(1, amount - fixed)
        return jnp.zeros((amount,), jnp.int32).at[ranking[jnp.where(places < fixed, places, shifted)]].set(jnp.asarray(lengths, jnp.int32))

    lengths = jnp.where(number % 4 == 0, named(crowded, number // 4), named(common, number - number // 4 - 1))
    mixed = jax.random.permutation(jax.random.fold_in(own, 3), amount)
    source_of, taker = mixed[0:amount // 2 * 2:2], mixed[1:amount // 2 * 2:2]
    room = jnp.minimum(lengths[source_of] - 1, most - lengths[taker]) // 2
    room = jnp.where((source_of == ranking[0]) | (taker == ranking[0]) | (lengths[taker] == 0), 0, jnp.maximum(room, 0))
    shifted = jax.random.randint(jax.random.fold_in(own, 4), (amount // 2,), 0, 1 << 20) % (room + 1)
    lengths = lengths.at[source_of].add(-shifted).at[taker].add(shifted)
    items = jnp.searchsorted(jnp.cumsum(lengths), jnp.arange(rows * top), side="right").astype(jnp.int32)
    listing = items.reshape(top, rows).T
    listing = listing[jax.random.permutation(jax.random.fold_in(own, 1), rows)]
    rotation = jax.random.randint(jax.random.fold_in(own, 2), (rows, 1), 0, top)
    return jnp.take_along_axis(listing, (jnp.arange(top)[None, :] + rotation) % top, axis=1)


def shares(amount, total, reach, skew, full):
    portions = [(1 << 20) // math.isqrt(grade ** skew) + 1 for grade in range(1, amount + 1)]
    largest = reach if full else min(reach, max(-(-total // amount), total * portions[0] // sum(portions)))
    least = 1 if total - largest >= amount - 1 else 0
    holding, spare = [largest] + [least] * (amount - 1), total - largest - least * (amount - 1)
    while spare > 0:
        candidates = [i for i in range(1, amount) if holding[i] < largest] or [i for i in range(1, amount) if holding[i] < reach]
        whole, left = sum([portions[i] for i in candidates]), spare
        for i in candidates:
            more = min(reach - holding[i], max(1, left * portions[i] // whole), spare)
            holding[i] = holding[i] + more
            spare = spare - more
    return np.array(holding)


def gaussian(stream_key, extent, scale, most, cuts=(), held_as=jnp.bfloat16):
    gain = levels(stream_key, extent, cuts, -0.22, 0.18) if cuts else 1.0
    entries = jax.random.normal(stream_key, extent, jnp.float32) * scale * gain
    return jnp.minimum(jnp.maximum(entries, -most), most).astype(held_as)


def setup_inputs(seed: int = 0) -> dict:
    key_of = jax.random.split(jax.random.key(seed), 14)
    tokens = gaussian(key_of[0], (TOKENS, D), 1.0, 6.0, ((0, 2), (1, 16)))
    ssm_input = gaussian(key_of[1], (TOKENS, D_INNER), 1.0, 6.0, ((0, 2), (1, 16)))
    in_b = gaussian(key_of[2], (TOKENS, NSTATE), (NSTATE ** -0.25), 1.75, ((0, 2),))
    in_c = gaussian(key_of[3], (TOKENS, NSTATE), (NSTATE ** -0.25), 1.75, ((0, 2),))
    decay_log = draw_decay_log(jax.random.fold_in(key_of[13], 71), 0)
    skip_gain = jnp.clip(1.0 + 0.18 * jax.random.normal(key_of[5], (HEADS,), jnp.float32), 0.1, 1.9)
    out_proj = gaussian(key_of[6], (D_INNER, D), D_INNER ** -0.5, 0.046875, ((0, 16), (1, 2)))
    norm_gain = jnp.clip(1.0 + 0.18 * jax.random.normal(key_of[7], (D,), jnp.float32), 0.1, 1.9)
    routes_keys = jax.random.split(jax.random.fold_in(key_of[8], 1), TOKENS // TOK_CTX)
    routes_turns = jax.random.permutation(jax.random.fold_in(key_of[8], 3), TOKENS // TOK_CTX)
    routes = jax.vmap(lambda own, number: assign_block(jax.random.fold_in(key_of[8], 2), own, number, TOK_CTX, EXPERTS, 2, MOST, 2))(routes_keys, routes_turns).reshape((TOKENS, 2))
    route_gate = jnp.clip(0.2 + 0.8 * jax.random.uniform(key_of[9], (TOKENS, 2), jnp.float32) ** levels(key_of[9], (TOKENS, 2), ((0, 2),), -0.2, 0.2), 0.2, 1.0)
    w_gate = gaussian(key_of[10], (EXPERTS, D, FF), D ** -0.5, 0.0625, ((0, 4), (2, 8)))
    w_up = gaussian(key_of[11], (EXPERTS, D, FF), D ** -0.5, 0.0625, ((0, 4), (2, 8)))
    w_down = gaussian(key_of[12], (EXPERTS, FF, D), FF ** -0.5, 0.0546875, ((0, 4), (1, 8)))
    return {"tokens": tokens, "ssm_input": ssm_input, "in_b": in_b, "in_c": in_c, "decay_log": decay_log, "skip_gain": skip_gain, "out_proj": out_proj, "norm_gain": norm_gain, "routes": routes, "route_gate": route_gate, "w_gate": w_gate, "w_up": w_up, "w_down": w_down}


def block_terms(ssm_input, in_b, in_c, decay_log):
    length = decay_log.shape[0]
    heads_here = decay_log.shape[1]
    width = ssm_input.shape[1] // heads_here
    values = ssm_input.astype(jnp.float32).reshape(length, heads_here, width)
    cumulative = jnp.cumsum(decay_log, axis=0)
    inflow = jnp.sqrt(-jnp.expm1(2.0 * decay_log))
    intersection = jnp.dot(in_c, in_b.T, preferred_element_type=jnp.float32)
    causal = jnp.arange(length)[:, None] >= jnp.arange(length)[None, :]
    spread = cumulative[:, None, :] - cumulative[None, :, :]
    fading = jnp.where(causal[:, :, None], jnp.exp(jnp.minimum(spread, 0.0)), 0.0)
    mixing = intersection[:, :, None] * fading * inflow[None, :, :]
    within = jnp.einsum('tsh,shp->thp', mixing, values, precision=lax.Precision.HIGHEST)
    tail = jnp.exp(cumulative[-1][None, :] - cumulative) * inflow
    state_here = jnp.einsum('sn,sh,shp->hnp', in_b.astype(jnp.float32), tail, values, precision=lax.Precision.HIGHEST)
    return (within, state_here, cumulative, values)

def finish_heads(within, carried, cumulative, values, in_c, skip_gain):
    outer = jnp.einsum('tn,hnp->thp', in_c.astype(jnp.float32), carried, precision=lax.Precision.HIGHEST)
    result = within + jnp.exp(cumulative)[:, :, None] * outer + skip_gain[None, :, None] * values
    return result.reshape(result.shape[0], -1).astype(jnp.bfloat16)

def route_tables(routes, route_gate, experts, most):
    onehot = (routes[:, :, None] == jnp.arange(experts, dtype=jnp.int32)[None, None, :]).astype(jnp.int32)
    flat = onehot.reshape(-1, experts)
    before = jnp.cumsum(flat, axis=0, dtype=jnp.int32) - flat
    slot = lax.optimization_barrier(jnp.sum(before * flat, axis=1, dtype=jnp.int32)).reshape(routes.shape)
    target = routes * most + slot
    columns = jnp.arange(experts * most, dtype=jnp.int32)
    hits = target[:, :, None] == columns[None, None, :]
    dispatch = jnp.any(hits, axis=1).T.astype(jnp.bfloat16)
    combine = lax.optimization_barrier(jnp.sum(jnp.where(hits, route_gate[:, :, None], 0.0), axis=1))
    return (dispatch, combine)

def reference(tokens, ssm_input, in_b, in_c, decay_log, skip_gain, out_proj, norm_gain, routes, route_gate, w_gate, w_up, w_down):

    def advance(carried, block):
        x_block, b_block, c_block, a_block = block
        within, state_here, cumulative, values = block_terms(x_block, b_block, c_block, a_block)
        mixed = finish_heads(within, carried, cumulative, values, c_block, skip_gain)
        carried = jnp.exp(cumulative[-1])[:, None, None] * carried + state_here
        return (carried, mixed)
    begin = jnp.zeros((HEADS, NSTATE, HEAD_DIM), jnp.float32)
    blocks = (ssm_input.reshape(N_CTX, TOK_CTX, D_INNER), in_b.reshape(N_CTX, TOK_CTX, NSTATE), in_c.reshape(N_CTX, TOK_CTX, NSTATE), decay_log.reshape(N_CTX, TOK_CTX, HEADS))
    _, mixed = lax.scan(advance, begin, blocks)
    mixed = mixed.reshape(TOKENS, D_INNER)
    groups = N_STATE * N_EXPERT
    group_rows = D_INNER // groups

    def add_group(index, accum):
        offset = (index * group_rows).astype(jnp.int32)
        product = jnp.dot(lax.dynamic_slice_in_dim(mixed, offset, group_rows, 1), lax.dynamic_slice_in_dim(out_proj, offset, group_rows, 0), preferred_element_type=jnp.float32)
        rounded = lax.optimization_barrier(product.astype(jnp.bfloat16))
        return accum + rounded.astype(jnp.float32)
    mixer_out = lax.fori_loop(0, groups, add_group, jnp.zeros((TOKENS, D), jnp.float32))
    resid = (tokens.astype(jnp.float32) + mixer_out).astype(jnp.bfloat16)
    wide = resid.astype(jnp.float32)
    scale = lax.rsqrt(lax.optimization_barrier(jnp.mean(wide * wide, axis=1)) + 1e-05)
    normed = (wide * scale[:, None] * norm_gain[None, :]).astype(jnp.bfloat16)
    dispatch, combine = jax.vmap(lambda r, g: route_tables(r, g, EXPERTS, MOST))(routes.reshape(N_CTX, TOK_CTX, 2), route_gate.reshape(N_CTX, TOK_CTX, 2))
    gathered = jnp.einsum('cjt,ctd->cjd', dispatch.astype(jnp.float32), normed.reshape(N_CTX, TOK_CTX, D).astype(jnp.float32), precision=lax.Precision.HIGHEST).astype(jnp.bfloat16)
    per_expert = gathered.reshape(N_CTX, EXPERTS, MOST, D).transpose(1, 0, 2, 3).reshape(EXPERTS, N_CTX * MOST, D)
    hidden_groups = N_CTX * N_STATE
    group_width = FF // hidden_groups

    def run_expert(operands):
        rows, gate_weight, up_weight, down_weight = operands
        gate_value = jnp.dot(rows, gate_weight, preferred_element_type=jnp.float32)
        up_value = jnp.dot(rows, up_weight, preferred_element_type=jnp.float32)
        hidden = (jax.nn.silu(gate_value) * up_value).astype(jnp.bfloat16)

        def add_hidden(index, accum):
            offset = (index * group_width).astype(jnp.int32)
            product = jnp.dot(lax.dynamic_slice_in_dim(hidden, offset, group_width, 1), lax.dynamic_slice_in_dim(down_weight, offset, group_width, 0), preferred_element_type=jnp.float32)
            rounded = lax.optimization_barrier(product.astype(jnp.bfloat16))
            return accum + rounded.astype(jnp.float32)
        summed = lax.fori_loop(0, hidden_groups, add_hidden, jnp.zeros((rows.shape[0], D), jnp.float32))
        return summed.astype(jnp.bfloat16)
    outputs = lax.map(run_expert, (per_expert, w_gate, w_up, w_down))
    returned = outputs.reshape(EXPERTS, N_CTX, MOST, D).transpose(1, 0, 2, 3).reshape(N_CTX, EXPERTS * MOST, D)
    combined = jnp.einsum('ctj,cjd->ctd', combine, returned.astype(jnp.float32), precision=lax.Precision.HIGHEST)
    return (wide + combined.reshape(TOKENS, D)).astype(jnp.bfloat16)
```

```python
import functools
import math

import jax
import jax.numpy as jnp
from jax import lax
from jax.experimental import pallas as pl
from jax.experimental.pallas import tpu as pltpu
from jax.sharding import PartitionSpec as P

MOST = 80
norm_epsilon = 1e-05
MESH = pl.DeviceIdType.MESH
HIGHEST = lax.Precision.HIGHEST
VMEM_SPEC = pl.BlockSpec(memory_space=pltpu.VMEM)


def digits_of(axis, size):
    if size > 2 and size % 2 == 0 and axis == "expert":
        return [(axis, 1, 2), (axis, 2, size // 2)]
    return [(axis, 1, size)]


def value_of(digit):
    axis, stride, size = digit
    return lax.rem(lax.axis_index(axis) // stride, size)


def peer_of(digit, step):
    axis, stride, size = digit
    mine = value_of(digit)
    other = lax.rem(mine + step, size)
    return other, {axis: lax.axis_index(axis) + (other - mine) * stride}


def greet(digits):
    barrier = pltpu.get_barrier_semaphore()
    count = 0
    for digit in digits:
        for step in range(1, digit[2]):
            pl.semaphore_signal(barrier, inc=1, device_id=peer_of(digit, step)[1], device_id_type=MESH)
            count += 1
    pl.semaphore_wait(barrier, count)


def gather_kernel(jobs, used, count, *refs):
    ins, outs = refs[:count], refs[count : 2 * count]
    local_sem, send_sem, recv_sem = refs[2 * count :]
    greet(used)
    locals_ = []
    for i in range(count):
        dims = next(job[1] for job in jobs if job[0] == i)
        place = tuple(value_of(d) for d in dims)
        copy = pltpu.make_async_copy(ins[i], outs[i].at[place], local_sem.at[i])
        copy.start()
        locals_.append(copy)
    number = 0
    stages = max(len(job[2]) for job in jobs)
    sends, waiting = [], {}
    for stage in range(stages):
        for j, (i, dims, order, columns) in enumerate(jobs):
            for copy in waiting.pop(j, ()):
                copy.wait_recv()
            if stage >= len(order):
                continue
            digit = order[stage]
            done = order[:stage]
            tail = (slice(None), pl.ds(*columns))
            place = tuple(slice(None) if d in done else value_of(d) for d in dims) + tail
            copies = []
            for step in range(1, digit[2]):
                copy = pltpu.make_async_remote_copy(
                    src_ref=ins[i].at[tail] if stage == 0 else outs[i].at[place],
                    dst_ref=outs[i].at[place],
                    send_sem=send_sem.at[number],
                    recv_sem=recv_sem.at[number],
                    device_id=peer_of(digit, step)[1],
                    device_id_type=MESH,
                )
                copy.start()
                number += 1
                copies.append(copy)
            waiting[j] = copies
            sends += copies
        if stage == 0:
            for copy in locals_:
                copy.wait()
    for copies in waiting.values():
        for copy in copies:
            copy.wait_recv()
    for copy in sends:
        copy.wait_send()


def gather(arrays, jobs, ident):
    used, total = [], 0
    for _, _, order, _ in jobs:
        for digit in order:
            total += digit[2] - 1
            if digit not in used:
                used.append(digit)
    outs = []
    for i, array in enumerate(arrays):
        dims = next(job[1] for job in jobs if job[0] == i)
        outs.append(jax.ShapeDtypeStruct(tuple(d[2] for d in dims) + array.shape, array.dtype))
    return pl.pallas_call(
        functools.partial(gather_kernel, jobs, used, len(arrays)),
        out_shape=outs,
        in_specs=[VMEM_SPEC] * len(arrays),
        out_specs=[VMEM_SPEC] * len(arrays),
        scratch_shapes=[
            pltpu.SemaphoreType.DMA((len(arrays),)),
            pltpu.SemaphoreType.DMA((total,)),
            pltpu.SemaphoreType.DMA((total,)),
        ],
        compiler_params=pltpu.CompilerParams(
            collective_id=ident, has_side_effects=True, vmem_limit_bytes=56 << 20
        ),
        name=f"gather{ident}",
    )(*arrays)


def scatter_kernel(dims, parts, x_ref, out_ref, *refs):
    send_sem, recv_sem = refs[-2:]
    buffers = refs[:-2]
    greet(dims)
    number = 0
    stages = len(dims)
    sends, state = [], []
    cursor = 0
    for order, r0, rows, c0, columns in parts:
        state.append([x_ref, list(dims), (pl.ds(r0, rows), pl.ds(c0, columns)), cursor])
        cursor += 2 * stages - 1
    for stage in range(stages):
        pending = []
        for p, (order, r0, rows, c0, columns) in enumerate(parts):
            source, left, tail, base = state[p]
            digit = order[stage]
            at = left.index(digit)
            landing = buffers[base + 2 * stage]
            copies = []
            for step in range(1, digit[2]):
                other, target = peer_of(digit, step)
                place = tuple(other if k == at else slice(None) for k in range(len(left))) + tail
                copy = pltpu.make_async_remote_copy(
                    src_ref=source.at[place],
                    dst_ref=landing.at[step - 1],
                    send_sem=send_sem.at[number],
                    recv_sem=recv_sem.at[number],
                    device_id=target,
                    device_id_type=MESH,
                )
                copy.start()
                number += 1
                copies.append(copy)
            sends += copies
            pending.append(copies)
        for p, (order, r0, rows, c0, columns) in enumerate(parts):
            source, left, tail, base = state[p]
            digit = order[stage]
            at = left.index(digit)
            landing = buffers[base + 2 * stage]
            rest = left[:at] + left[at + 1 :]
            last = stage == stages - 1
            target = out_ref if last else buffers[base + 2 * stage + 1]
            mine = value_of(digit)
            for copy in pending[p]:
                copy.wait_recv()
            lead = [d[2] for d in rest]

            def add(index, _, source=source, landing=landing, target=target, lead=lead, at=at, mine=mine, tail=tail, last=last, size=digit[2]):
                where, scale = [], math.prod(lead)
                for n in lead:
                    scale //= n
                    where.append((index // scale) % n)
                where = tuple(where)
                total = source[where[:at] + (mine,) + where[at:] + tail].astype(jnp.float32)
                for k in range(size - 1):
                    total = total + landing[(k,) + where].astype(jnp.float32)
                if last:
                    target[tail_out] = total
                else:
                    target[where] = total.astype(target.dtype)
                return 0

            tail_out = (pl.ds(r0, rows), pl.ds(c0, columns))
            count = math.prod(lead)
            if count == 1:
                add(0, 0)
            else:
                lax.fori_loop(0, count, add, 0)
            state[p] = [target, rest, (slice(None), slice(None)), base]
    for copy in sends:
        copy.wait_send()


def scatter(x, dims, parts, ident):
    scratch, total = [], 0
    for order, r0, rows, c0, columns in parts:
        left = list(dims)
        for stage, digit in enumerate(order):
            left.remove(digit)
            rest = tuple(d[2] for d in left) + (rows, columns)
            scratch.append(pltpu.VMEM((digit[2] - 1,) + rest, x.dtype))
            total += digit[2] - 1
            if stage < len(order) - 1:
                scratch.append(pltpu.VMEM(rest, x.dtype))
    return pl.pallas_call(
        functools.partial(scatter_kernel, dims, parts),
        out_shape=jax.ShapeDtypeStruct(x.shape[len(dims) :], jnp.float32),
        in_specs=[VMEM_SPEC],
        out_specs=VMEM_SPEC,
        scratch_shapes=scratch
        + [pltpu.SemaphoreType.DMA((total,)), pltpu.SemaphoreType.DMA((total,))],
        compiler_params=pltpu.CompilerParams(
            collective_id=ident, has_side_effects=True, vmem_limit_bytes=56 << 20
        ),
        name=f"scatter{ident}",
    )(x)


def thirds(total, unit):
    first = max(unit, (total * 3 // 8) // unit * unit)
    return [(0, first), (first, first), (2 * first, total - 2 * first)]


def block_terms(ssm_input, in_b, in_c, decay_log):
    length = decay_log.shape[0]
    heads_here = decay_log.shape[1]
    width = ssm_input.shape[1] // heads_here
    values = ssm_input.astype(jnp.float32).reshape(length, heads_here, width)
    cumulative = jnp.cumsum(decay_log, axis=0)
    inflow = jnp.sqrt(-jnp.expm1(2.0 * decay_log))
    intersection = jnp.dot(in_c, in_b.T, preferred_element_type=jnp.float32)
    causal = jnp.arange(length)[:, None] >= jnp.arange(length)[None, :]
    spread = cumulative[:, None, :] - cumulative[None, :, :]
    fading = jnp.where(causal[:, :, None], jnp.exp(jnp.minimum(spread, 0.0)), 0.0)
    mixing = intersection[:, :, None] * fading * inflow[None, :, :]
    within = jnp.einsum("tsh,shp->thp", mixing, values, precision=HIGHEST)
    tail = jnp.exp(cumulative[-1][None, :] - cumulative) * inflow
    state_here = jnp.einsum(
        "sn,sh,shp->hnp", in_b.astype(jnp.float32), tail, values, precision=HIGHEST
    )
    return (within, state_here, cumulative, values)


def finish_heads(within, carried, cumulative, values, in_c, skip_gain):
    result = within + skip_gain[None, :, None] * values
    if carried is not None:
        outer = jnp.einsum("tn,hnp->thp", in_c.astype(jnp.float32), carried, precision=HIGHEST)
        result = result + jnp.exp(cumulative)[:, :, None] * outer
    return result.reshape(result.shape[0], -1).astype(jnp.bfloat16)


def shards(
    tokens,
    ssm_input,
    in_b,
    in_c,
    decay_log,
    skip_gain,
    out_proj,
    norm_gain,
    routes,
    route_gate,
    w_gate,
    w_up,
    w_down,
):
    n_ctx, n_state, n_expert = (lax.axis_size(a) for a in ("ctx", "state", "expert"))
    ctx_at, state_at, expert_at = (lax.axis_index(a) for a in ("ctx", "state", "expert"))
    length, block = tokens.shape
    count = n_ctx * length
    groups = n_state * n_expert
    half = out_proj.shape[1]
    width = half * n_ctx
    ctx = digits_of("ctx", n_ctx)
    state = digits_of("state", n_state)
    expert = digits_of("expert", n_expert)
    expert_down = expert[::-1]

    raw = [ssm_input, in_b, in_c, decay_log, tokens, routes, route_gate, norm_gain[None, :]]
    jobs = [(i, ctx, ctx, (0, a.shape[1])) for i, a in enumerate(raw[:-1])]
    jobs.append((len(raw) - 1, state + expert_down, state + expert_down, (0, block)))
    all_ssm, all_b, all_c, all_decay, all_tokens, all_routes, all_gate, gain = gather(raw, jobs, 0)
    gain = gain.reshape(n_ctx, 1, half)

    carried, mixed = None, []
    for c in range(n_ctx):
        within, state_here, cumulative, values = block_terms(
            all_ssm[c], all_b[c], all_c[c], all_decay[c]
        )
        mixed.append(finish_heads(within, carried, cumulative, values, all_c[c], skip_gain))
        if carried is None:
            carried = state_here
        else:
            carried = jnp.exp(cumulative[-1])[:, None, None] * carried + state_here
    all_mixed = jnp.concatenate(mixed, axis=0)

    product = jnp.dot(all_mixed, out_proj, preferred_element_type=jnp.float32)
    columns_here = half // block
    own = state_at * n_expert + expert_at - ctx_at * columns_here
    mine = (jnp.arange(columns_here, dtype=jnp.int32) == own)[:, None, None]
    token_rows = all_tokens.reshape(count, block).astype(jnp.float32)
    added = jnp.where(jnp.repeat(jnp.arange(columns_here, dtype=jnp.int32) == own, block)[None, :],
                      jnp.tile(token_rows, (1, columns_here)), 0.0)
    summands = (product + added).astype(jnp.bfloat16)
    rows = count // groups
    dims = state + expert_down
    summands = summands.reshape(tuple(d[2] for d in dims) + (rows, half))
    side = expert[1:]
    orders = [expert + state, expert[:1] + state + side]
    parts = [(order, 0, rows, k * (half // 2), half // 2) for k, order in enumerate(orders)]
    resid_piece = scatter(summands, dims, parts, 1).astype(jnp.bfloat16)

    whole = ctx + dims
    core = expert[:1]
    orders = [state + ctx + side + core, state + side + ctx + core, side + ctx + state + core]
    jobs = [(0, whole, order, cut) for order, cut in zip(orders, thirds(half, 128))]
    (resid,) = gather([resid_piece], jobs, 2)
    resid = resid.reshape(n_ctx, count, half)

    wide = resid.astype(jnp.float32)
    scale = lax.rsqrt(jnp.sum(wide * wide, axis=(0, 2)) / width + norm_epsilon)

    routed = all_routes == expert_at
    chosen = jnp.any(routed, axis=2)
    weight = jnp.sum(jnp.where(routed, all_gate, 0.0), axis=2).reshape(count)
    flags = chosen.astype(jnp.bfloat16)
    earlier = (jnp.arange(length)[:, None] < jnp.arange(length)[None, :]).astype(jnp.bfloat16)
    slot = jnp.dot(flags, earlier, preferred_element_type=jnp.float32).astype(jnp.int32)
    target = jnp.where(chosen, slot + MOST * jnp.arange(n_ctx, dtype=jnp.int32)[:, None], -1)
    hits = jnp.arange(n_ctx * MOST, dtype=jnp.int32)[:, None] == target.reshape(1, count)
    dispatch = hits.astype(jnp.bfloat16)
    slot_weight = jnp.sum(jnp.where(hits, weight[None, :], 0.0), axis=1)
    slot_scale = jnp.sum(jnp.where(hits, scale[None, :], 0.0), axis=1)

    picked = jnp.einsum("rt,ctd->crd", dispatch, resid, preferred_element_type=jnp.float32)
    entering = (picked * slot_scale[None, :, None] * gain).astype(jnp.bfloat16)
    gate_parts = w_gate.reshape(n_ctx, half, w_gate.shape[2])
    up_parts = w_up.reshape(n_ctx, half, w_up.shape[2])
    gate_value = jnp.einsum("crd,cdh->rh", entering, gate_parts, preferred_element_type=jnp.float32)
    up_value = jnp.einsum("crd,cdh->rh", entering, up_parts, preferred_element_type=jnp.float32)
    hidden = (jax.nn.silu(gate_value) * up_value * slot_weight[:, None]).astype(jnp.bfloat16)
    terms = jnp.dot(hidden, w_down[0], preferred_element_type=jnp.float32).astype(jnp.bfloat16)
    spread = jnp.einsum(
        "rt,rgd->gtd", dispatch, terms.reshape(-1, groups, block), preferred_element_type=jnp.float32
    ).astype(jnp.bfloat16)
    dims = state + expert_down + ctx
    spread = spread.reshape(tuple(d[2] for d in dims) + (length, block))
    orders = [core + side + ctx + state, core + ctx + side + state, core + state + side + ctx]
    parts = [(order, r0, n, 0, block) for order, (r0, n) in zip(orders, thirds(length, 16))]
    combined = scatter(spread, dims, parts, 3)

    position = (state_at * n_expert + expert_at) * block
    own_resid = lax.dynamic_slice(
        resid, (position // half, ctx_at * length, position % half), (1, length, block)
    )[0]
    return (own_resid.astype(jnp.float32) + combined).astype(jnp.bfloat16)


def solution(mesh):
    in_specs = (
        P("ctx", ("state", "expert")),
        P("ctx", ("state", "expert")),
        P("ctx", None),
        P("ctx", None),
        P("ctx", ("state", "expert")),
        P(("state", "expert")),
        P(("state", "expert"), "ctx"),
        P(("state", "expert")),
        P("ctx", None),
        P("ctx", None),
        P("expert", None, ("ctx", "state")),
        P("expert", None, ("ctx", "state")),
        P("expert", ("ctx", "state"), None),
    )
    out_specs = P("ctx", ("state", "expert"))
    return jax.shard_map(shards, mesh=mesh, in_specs=in_specs, out_specs=out_specs, check_vma=False)
```

```python
import functools
import math

import jax
import jax.numpy as jnp
from jax import lax
from jax.experimental import pallas as pl
from jax.experimental.pallas import tpu as pltpu
from jax.sharding import PartitionSpec as P

MOST = 80
norm_epsilon = 1e-05
MESH = pl.DeviceIdType.MESH
HIGHEST = lax.Precision.HIGHEST
VMEM_SPEC = pl.BlockSpec(memory_space=pltpu.VMEM)


def digits_of(axis, size):
    if size > 2 and size % 2 == 0 and axis == "expert":
        return [(axis, 1, 2), (axis, 2, size // 2)]
    return [(axis, 1, size)]


def value_of(digit):
    axis, stride, size = digit
    return lax.rem(lax.axis_index(axis) // stride, size)


def peer_of(digit, step):
    axis, stride, size = digit
    mine = value_of(digit)
    other = lax.rem(mine + step, size)
    return other, {axis: lax.axis_index(axis) + (other - mine) * stride}


def greet(digits):
    barrier = pltpu.get_barrier_semaphore()
    count = 0
    for digit in digits:
        for step in range(1, digit[2]):
            pl.semaphore_signal(barrier, inc=1, device_id=peer_of(digit, step)[1], device_id_type=MESH)
            count += 1
    pl.semaphore_wait(barrier, count)


def gather_kernel(jobs, used, count, *refs):
    ins, outs = refs[:count], refs[count : 2 * count]
    local_sem, send_sem, recv_sem = refs[2 * count :]
    greet(used)
    locals_ = []
    for i in range(count):
        dims = next(job[1] for job in jobs if job[0] == i)
        place = tuple(value_of(d) for d in dims)
        copy = pltpu.make_async_copy(ins[i], outs[i].at[place], local_sem.at[i])
        copy.start()
        locals_.append(copy)
    number = 0
    stages = max(len(job[2]) for job in jobs)
    sends, waiting = [], {}
    for stage in range(stages):
        for j, (i, dims, order, columns) in enumerate(jobs):
            for copy in waiting.pop(j, ()):
                copy.wait_recv()
            if stage >= len(order):
                continue
            digit = order[stage]
            done = order[:stage]
            tail = (slice(None), pl.ds(*columns))
            place = tuple(slice(None) if d in done else value_of(d) for d in dims) + tail
            copies = []
            for step in range(1, digit[2]):
                copy = pltpu.make_async_remote_copy(
                    src_ref=ins[i].at[tail] if stage == 0 else outs[i].at[place],
                    dst_ref=outs[i].at[place],
                    send_sem=send_sem.at[number],
                    recv_sem=recv_sem.at[number],
                    device_id=peer_of(digit, step)[1],
                    device_id_type=MESH,
                )
                copy.start()
                number += 1
                copies.append(copy)
            waiting[j] = copies
            sends += copies
        if stage == 0:
            for copy in locals_:
                copy.wait()
    for copies in waiting.values():
        for copy in copies:
            copy.wait_recv()
    for copy in sends:
        copy.wait_send()


def gather(arrays, jobs, ident):
    used, total = [], 0
    for _, _, order, _ in jobs:
        for digit in order:
            total += digit[2] - 1
            if digit not in used:
                used.append(digit)
    outs = []
    for i, array in enumerate(arrays):
        dims = next(job[1] for job in jobs if job[0] == i)
        outs.append(jax.ShapeDtypeStruct(tuple(d[2] for d in dims) + array.shape, array.dtype))
    return pl.pallas_call(
        functools.partial(gather_kernel, jobs, used, len(arrays)),
        out_shape=outs,
        in_specs=[VMEM_SPEC] * len(arrays),
        out_specs=[VMEM_SPEC] * len(arrays),
        scratch_shapes=[
            pltpu.SemaphoreType.DMA((len(arrays),)),
            pltpu.SemaphoreType.DMA((total,)),
            pltpu.SemaphoreType.DMA((total,)),
        ],
        compiler_params=pltpu.CompilerParams(
            collective_id=ident, has_side_effects=True, vmem_limit_bytes=56 << 20
        ),
        name=f"gather{ident}",
    )(*arrays)


def scatter_kernel(dims, parts, x_ref, out_ref, *refs):
    send_sem, recv_sem = refs[-2:]
    buffers = refs[:-2]
    greet(dims)
    stages = len(dims)
    sends, pending, state = [], {}, []
    for p, (order, r0, rows, c0, columns) in enumerate(parts):
        tail = (pl.ds(r0, rows), pl.ds(c0, columns))
        state.append((x_ref, list(dims), tail, p * (2 * stages - 1)))

    def begin(p, stage):
        source, left, tail, base = state[p]
        digit = parts[p][0][stage]
        at = left.index(digit)
        pending[p] = []
        for step in range(1, digit[2]):
            other, target = peer_of(digit, step)
            place = tuple(other if k == at else slice(None) for k in range(len(left))) + tail
            copy = pltpu.make_async_remote_copy(
                src_ref=source.at[place],
                dst_ref=buffers[base + 2 * stage].at[step - 1],
                send_sem=send_sem.at[len(sends)],
                recv_sem=recv_sem.at[len(sends)],
                device_id=target,
                device_id_type=MESH,
            )
            copy.start()
            sends.append(copy)
            pending[p].append(copy)

    def finish(p, stage):
        order, r0, rows, c0, columns = parts[p]
        source, left, tail, base = state[p]
        digit = order[stage]
        at = left.index(digit)
        rest = left[:at] + left[at + 1 :]
        landing = buffers[base + 2 * stage]
        last = stage == stages - 1
        target = out_ref if last else buffers[base + 2 * stage + 1]
        mine = value_of(digit)
        for copy in pending[p]:
            copy.wait_recv()
        count = math.prod(d[2] for d in rest)

        def add(index, _):
            where, scale = [], count
            for d in rest:
                scale //= d[2]
                where.append((index // scale) % d[2])
            where = tuple(where)
            total = source[where[:at] + (mine,) + where[at:] + tail].astype(jnp.float32)
            for k in range(digit[2] - 1):
                total = total + landing[(k,) + where].astype(jnp.float32)
            spot = (pl.ds(r0, rows), pl.ds(c0, columns)) if last else where
            target[spot] = total.astype(target.dtype)
            return 0

        if count == 1:
            add(0, 0)
        else:
            lax.fori_loop(0, count, add, 0)
        state[p] = (target, rest, (slice(None), slice(None)), base)

    for p in range(len(parts)):
        begin(p, 0)
    for stage in range(stages):
        for p in range(len(parts)):
            finish(p, stage)
            if stage < stages - 1:
                begin(p, stage + 1)
    for copy in sends:
        copy.wait_send()


def scatter(x, dims, parts, ident, kind):
    scratch, total = [], 0
    for order, r0, rows, c0, columns in parts:
        left = list(dims)
        for stage, digit in enumerate(order):
            left.remove(digit)
            rest = tuple(d[2] for d in left) + (rows, columns)
            scratch.append(pltpu.VMEM((digit[2] - 1,) + rest, x.dtype))
            total += digit[2] - 1
            if stage < len(order) - 1:
                scratch.append(pltpu.VMEM(rest, x.dtype))
    return pl.pallas_call(
        functools.partial(scatter_kernel, dims, parts),
        out_shape=jax.ShapeDtypeStruct(x.shape[len(dims) :], kind),
        in_specs=[VMEM_SPEC],
        out_specs=VMEM_SPEC,
        scratch_shapes=scratch
        + [pltpu.SemaphoreType.DMA((total,)), pltpu.SemaphoreType.DMA((total,))],
        compiler_params=pltpu.CompilerParams(
            collective_id=ident, has_side_effects=True, vmem_limit_bytes=56 << 20
        ),
        name=f"scatter{ident}",
    )(x)


def thirds(total, unit):
    first = max(unit, (total * 3 // 8) // unit * unit)
    return [(0, first), (first, first), (2 * first, total - 2 * first)]


def halves(total):
    first = max(128, (total // 2 + 127) // 128 * 128)
    return [(0, first), (first, total - first)]


def block_terms(ssm_input, in_b, in_c, decay_log):
    length = decay_log.shape[0]
    heads_here = decay_log.shape[1]
    width = ssm_input.shape[1] // heads_here
    values = ssm_input.astype(jnp.float32).reshape(length, heads_here, width)
    cumulative = jnp.cumsum(decay_log, axis=0)
    inflow = jnp.sqrt(-jnp.expm1(2.0 * decay_log))
    intersection = jnp.dot(in_c, in_b.T, preferred_element_type=jnp.float32)
    causal = jnp.arange(length)[:, None] >= jnp.arange(length)[None, :]
    spread = cumulative[:, None, :] - cumulative[None, :, :]
    fading = jnp.where(causal[:, :, None], jnp.exp(jnp.minimum(spread, 0.0)), 0.0)
    mixing = intersection[:, :, None] * fading * inflow[None, :, :]
    within = jnp.einsum("tsh,shp->thp", mixing, values, precision=HIGHEST)
    tail = jnp.exp(cumulative[-1][None, :] - cumulative) * inflow
    state_here = jnp.einsum(
        "sn,sh,shp->hnp", in_b.astype(jnp.float32), tail, values, precision=HIGHEST
    )
    return (within, state_here, cumulative, values)


def finish_heads(within, carried, cumulative, values, in_c, skip_gain):
    result = within + skip_gain[None, :, None] * values
    if carried is not None:
        outer = jnp.einsum("tn,hnp->thp", in_c.astype(jnp.float32), carried, precision=HIGHEST)
        result = result + jnp.exp(cumulative)[:, :, None] * outer
    return result.reshape(result.shape[0], -1).astype(jnp.bfloat16)


def shards(
    tokens,
    ssm_input,
    in_b,
    in_c,
    decay_log,
    skip_gain,
    out_proj,
    norm_gain,
    routes,
    route_gate,
    w_gate,
    w_up,
    w_down,
):
    n_ctx, n_state, n_expert = (lax.axis_size(a) for a in ("ctx", "state", "expert"))
    ctx_at, state_at, expert_at = (lax.axis_index(a) for a in ("ctx", "state", "expert"))
    length, block = tokens.shape
    count = n_ctx * length
    groups = n_state * n_expert
    half = out_proj.shape[1]
    width = half * n_ctx
    ctx = digits_of("ctx", n_ctx)
    state = digits_of("state", n_state)
    expert = digits_of("expert", n_expert)
    expert_down = expert[::-1]

    heads, top = decay_log.shape[1], routes.shape[1]
    small = jnp.concatenate([decay_log.T, route_gate.T, routes.T.astype(jnp.float32)], axis=0)
    raw = [ssm_input, in_b, in_c, small, tokens]
    jobs = [(i, ctx, ctx, (0, a.shape[1])) for i, a in enumerate(raw)]
    all_ssm, all_b, all_c, all_small, all_tokens = gather(raw, jobs, 0)
    all_decay = all_small[:, :heads].transpose(0, 2, 1)
    all_gate = all_small[:, heads : heads + top].transpose(0, 2, 1)
    all_routes = all_small[:, heads + top :].transpose(0, 2, 1).astype(jnp.int32)

    carried, mixed = None, []
    for c in range(n_ctx):
        within, state_here, cumulative, values = block_terms(
            all_ssm[c], all_b[c], all_c[c], all_decay[c]
        )
        mixed.append(finish_heads(within, carried, cumulative, values, all_c[c], skip_gain))
        if carried is None:
            carried = state_here
        else:
            carried = jnp.exp(cumulative[-1])[:, None, None] * carried + state_here
    all_mixed = jnp.concatenate(mixed, axis=0)

    product = jnp.dot(all_mixed, out_proj, preferred_element_type=jnp.float32).astype(jnp.bfloat16)
    own = (state_at * n_expert + expert_at) * block - ctx_at * half
    held = jnp.logical_and(own >= 0, own < half)
    start = jnp.clip(own, 0, half - block)
    patch = lax.dynamic_slice(product, (0, start), (count, block)).astype(jnp.float32)
    patch = patch + jnp.where(held, all_tokens.reshape(count, block).astype(jnp.float32), 0.0)
    summands = lax.dynamic_update_slice(product, patch.astype(jnp.bfloat16), (0, start))
    rows = count // groups
    dims = state + expert_down
    summands = summands.reshape(tuple(d[2] for d in dims) + (rows, half))
    side = expert[1:]
    orders = [expert + state, expert[:1] + state + side]
    parts = [
        (order, 0, rows, k * (half // 2) + start, size)
        for start, size in halves(half // 2)
        for k, order in enumerate(orders)
    ]
    resid_piece = scatter(summands, dims, parts, 1, jnp.bfloat16)

    whole = ctx + dims
    core = expert[:1]
    orders = [state + ctx + side + core, state + side + ctx + core, side + ctx + state + core]
    cuts = [[(a + start, size) for start, size in halves(n)] for a, n in thirds(half, 128)]
    jobs = [(0, whole, order, cut[k]) for k in range(2) for order, cut in zip(orders, cuts)]
    spread_over = state + expert_down
    jobs.append((1, spread_over, spread_over, (0, block)))
    resid, gain = gather([resid_piece, norm_gain[None, :]], jobs, 2)
    gain = gain.reshape(n_ctx, 1, half)
    resid = resid.reshape(n_ctx, count, half)

    wide = resid.astype(jnp.float32)
    scale = lax.rsqrt(jnp.sum(wide * wide, axis=(0, 2)) / width + norm_epsilon)

    routed = all_routes == expert_at
    chosen = jnp.any(routed, axis=2)
    weight = jnp.sum(jnp.where(routed, all_gate, 0.0), axis=2).reshape(count)
    flags = chosen.astype(jnp.bfloat16)
    earlier = (jnp.arange(length)[:, None] < jnp.arange(length)[None, :]).astype(jnp.bfloat16)
    slot = jnp.dot(flags, earlier, preferred_element_type=jnp.float32).astype(jnp.int32)
    target = jnp.where(chosen, slot + MOST * jnp.arange(n_ctx, dtype=jnp.int32)[:, None], -1)
    hits = jnp.arange(n_ctx * MOST, dtype=jnp.int32)[:, None] == target.reshape(1, count)
    dispatch = hits.astype(jnp.bfloat16)
    slot_weight = jnp.sum(jnp.where(hits, weight[None, :], 0.0), axis=1)
    slot_scale = jnp.sum(jnp.where(hits, scale[None, :], 0.0), axis=1)

    picked = jnp.einsum("rt,ctd->crd", dispatch, resid, preferred_element_type=jnp.float32)
    entering = (picked * slot_scale[None, :, None] * gain).astype(jnp.bfloat16)
    gate_parts = w_gate.reshape(n_ctx, half, w_gate.shape[2])
    up_parts = w_up.reshape(n_ctx, half, w_up.shape[2])
    gate_value = jnp.einsum("crd,cdh->rh", entering, gate_parts, preferred_element_type=jnp.float32)
    up_value = jnp.einsum("crd,cdh->rh", entering, up_parts, preferred_element_type=jnp.float32)
    hidden = (jax.nn.silu(gate_value) * up_value * slot_weight[:, None]).astype(jnp.bfloat16)
    terms = jnp.dot(hidden, w_down[0], preferred_element_type=jnp.float32).astype(jnp.bfloat16)
    spread = jnp.einsum(
        "rt,rgd->gtd", dispatch, terms.reshape(-1, groups, block), preferred_element_type=jnp.float32
    ).astype(jnp.bfloat16)
    dims = state + expert_down + ctx
    spread = spread.reshape(tuple(d[2] for d in dims) + (length, block))
    orders = [core + side + ctx + state, core + ctx + side + state, core + state + side + ctx]
    parts = [
        (order, r0, n, start, size)
        for start, size in halves(block)
        for order, (r0, n) in zip(orders, thirds(length, 16))
    ]
    combined = scatter(spread, dims, parts, 3, jnp.float32)

    position = (state_at * n_expert + expert_at) * block
    own_resid = lax.dynamic_slice(
        resid, (position // half, ctx_at * length, position % half), (1, length, block)
    )[0]
    return (own_resid.astype(jnp.float32) + combined).astype(jnp.bfloat16)


def solution(mesh):
    in_specs = (
        P("ctx", ("state", "expert")),
        P("ctx", ("state", "expert")),
        P("ctx", None),
        P("ctx", None),
        P("ctx", ("state", "expert")),
        P(("state", "expert")),
        P(("state", "expert"), "ctx"),
        P(("state", "expert")),
        P("ctx", None),
        P("ctx", None),
        P("expert", None, ("ctx", "state")),
        P("expert", None, ("ctx", "state")),
        P("expert", ("ctx", "state"), None),
    )
    out_specs = P("ctx", ("state", "expert"))
    return jax.shard_map(shards, mesh=mesh, in_specs=in_specs, out_specs=out_specs, check_vma=False)
```

```python
import functools
import math

import jax
import jax.numpy as jnp
from jax import lax
from jax.experimental import pallas as pl
from jax.experimental.pallas import tpu as pltpu
from jax.sharding import PartitionSpec as P

MOST = 80
norm_epsilon = 1e-05
MESH = pl.DeviceIdType.MESH
HIGHEST = lax.Precision.HIGHEST
VMEM_SPEC = pl.BlockSpec(memory_space=pltpu.VMEM)


def digits_of(axis, size):
    if size > 2 and size % 2 == 0 and axis == "expert":
        return [(axis, 1, 2), (axis, 2, size // 2)]
    return [(axis, 1, size)]


def value_of(digit):
    axis, stride, size = digit
    return lax.rem(lax.axis_index(axis) // stride, size)


def peer_of(digit, step):
    axis, stride, size = digit
    mine = value_of(digit)
    other = lax.rem(mine + step, size)
    return other, {axis: lax.axis_index(axis) + (other - mine) * stride}


def greet(digits):
    barrier = pltpu.get_barrier_semaphore()
    count = 0
    for digit in digits:
        for step in range(1, digit[2]):
            pl.semaphore_signal(barrier, inc=1, device_id=peer_of(digit, step)[1], device_id_type=MESH)
            count += 1
    pl.semaphore_wait(barrier, count)


def gather_kernel(jobs, used, count, *refs):
    ins, outs = refs[:count], refs[count : 2 * count]
    local_sem, send_sem, recv_sem = refs[2 * count :]
    greet(used)
    locals_ = []
    for i in range(count):
        dims = next(job[1] for job in jobs if job[0] == i)
        place = tuple(value_of(d) for d in dims)
        copy = pltpu.make_async_copy(ins[i], outs[i].at[place], local_sem.at[i])
        copy.start()
        locals_.append(copy)
    number = 0
    stages = max(len(job[2]) for job in jobs)
    sends, waiting = [], {}
    for stage in range(stages):
        for j, (i, dims, order, columns) in enumerate(jobs):
            for copy in waiting.pop(j, ()):
                copy.wait_recv()
            if stage >= len(order):
                continue
            digit = order[stage]
            done = order[:stage]
            tail = (slice(None), pl.ds(*columns))
            place = tuple(slice(None) if d in done else value_of(d) for d in dims) + tail
            copies = []
            for step in range(1, digit[2]):
                copy = pltpu.make_async_remote_copy(
                    src_ref=ins[i].at[tail] if stage == 0 else outs[i].at[place],
                    dst_ref=outs[i].at[place],
                    send_sem=send_sem.at[number],
                    recv_sem=recv_sem.at[number],
                    device_id=peer_of(digit, step)[1],
                    device_id_type=MESH,
                )
                copy.start()
                number += 1
                copies.append(copy)
            waiting[j] = copies
            sends += copies
        if stage == 0:
            for copy in locals_:
                copy.wait()
    for copies in waiting.values():
        for copy in copies:
            copy.wait_recv()
    for copy in sends:
        copy.wait_send()


def gather(arrays, jobs, ident):
    used, total = [], 0
    for _, _, order, _ in jobs:
        for digit in order:
            total += digit[2] - 1
            if digit not in used:
                used.append(digit)
    outs = []
    for i, array in enumerate(arrays):
        dims = next(job[1] for job in jobs if job[0] == i)
        outs.append(jax.ShapeDtypeStruct(tuple(d[2] for d in dims) + array.shape, array.dtype))
    return pl.pallas_call(
        functools.partial(gather_kernel, jobs, used, len(arrays)),
        out_shape=outs,
        in_specs=[VMEM_SPEC] * len(arrays),
        out_specs=[VMEM_SPEC] * len(arrays),
        scratch_shapes=[
            pltpu.SemaphoreType.DMA((len(arrays),)),
            pltpu.SemaphoreType.DMA((total,)),
            pltpu.SemaphoreType.DMA((total,)),
        ],
        compiler_params=pltpu.CompilerParams(
            collective_id=ident, has_side_effects=True, vmem_limit_bytes=56 << 20
        ),
        name=f"gather{ident}",
    )(*arrays)


def scatter_kernel(dims, parts, x_ref, out_ref, *refs):
    send_sem, recv_sem = refs[-2:]
    buffers = refs[:-2]
    greet(dims)
    stages = len(dims)
    sends, pending, state = [], {}, []
    for p, (order, r0, rows, c0, columns) in enumerate(parts):
        tail = (pl.ds(r0, rows), pl.ds(c0, columns))
        state.append((x_ref, list(dims), tail, p * (2 * stages - 1)))

    def begin(p, stage):
        source, left, tail, base = state[p]
        digit = parts[p][0][stage]
        at = left.index(digit)
        pending[p] = []
        for step in range(1, digit[2]):
            other, target = peer_of(digit, step)
            place = tuple(other if k == at else slice(None) for k in range(len(left))) + tail
            copy = pltpu.make_async_remote_copy(
                src_ref=source.at[place],
                dst_ref=buffers[base + 2 * stage].at[step - 1],
                send_sem=send_sem.at[len(sends)],
                recv_sem=recv_sem.at[len(sends)],
                device_id=target,
                device_id_type=MESH,
            )
            copy.start()
            sends.append(copy)
            pending[p].append(copy)

    def finish(p, stage):
        order, r0, rows, c0, columns = parts[p]
        source, left, tail, base = state[p]
        digit = order[stage]
        at = left.index(digit)
        rest = left[:at] + left[at + 1 :]
        landing = buffers[base + 2 * stage]
        last = stage == stages - 1
        target = out_ref if last else buffers[base + 2 * stage + 1]
        mine = value_of(digit)
        for copy in pending[p]:
            copy.wait_recv()
        count = math.prod(d[2] for d in rest)

        def add(index, _):
            where, scale = [], count
            for d in rest:
                scale //= d[2]
                where.append((index // scale) % d[2])
            where = tuple(where)
            total = source[where[:at] + (mine,) + where[at:] + tail].astype(jnp.float32)
            for k in range(digit[2] - 1):
                total = total + landing[(k,) + where].astype(jnp.float32)
            spot = (pl.ds(r0, rows), pl.ds(c0, columns)) if last else where
            target[spot] = total.astype(target.dtype)
            return 0

        if count == 1:
            add(0, 0)
        else:
            lax.fori_loop(0, count, add, 0)
        state[p] = (target, rest, (slice(None), slice(None)), base)

    for p in range(len(parts)):
        begin(p, 0)
    for stage in range(stages):
        for p in range(len(parts)):
            finish(p, stage)
            if stage < stages - 1:
                begin(p, stage + 1)
    for copy in sends:
        copy.wait_send()


def scatter(x, dims, parts, ident, kind):
    scratch, total = [], 0
    for order, r0, rows, c0, columns in parts:
        left = list(dims)
        for stage, digit in enumerate(order):
            left.remove(digit)
            rest = tuple(d[2] for d in left) + (rows, columns)
            scratch.append(pltpu.VMEM((digit[2] - 1,) + rest, x.dtype))
            total += digit[2] - 1
            if stage < len(order) - 1:
                scratch.append(pltpu.VMEM(rest, x.dtype))
    return pl.pallas_call(
        functools.partial(scatter_kernel, dims, parts),
        out_shape=jax.ShapeDtypeStruct(x.shape[len(dims) :], kind),
        in_specs=[VMEM_SPEC],
        out_specs=VMEM_SPEC,
        scratch_shapes=scratch
        + [pltpu.SemaphoreType.DMA((total,)), pltpu.SemaphoreType.DMA((total,))],
        compiler_params=pltpu.CompilerParams(
            collective_id=ident, has_side_effects=True, vmem_limit_bytes=56 << 20
        ),
        name=f"scatter{ident}",
    )(x)


def thirds(total, unit):
    first = max(unit, (total * 3 // 8) // unit * unit)
    return [(0, first), (first, first), (2 * first, total - 2 * first)]


def halves(total):
    first = max(128, (total // 2 + 127) // 128 * 128)
    return [(0, first), (first, total - first)]


def block_terms(ssm_input, in_b, in_c, decay_log):
    length = decay_log.shape[0]
    heads_here = decay_log.shape[1]
    width = ssm_input.shape[1] // heads_here
    values = ssm_input.astype(jnp.float32).reshape(length, heads_here, width)
    cumulative = jnp.cumsum(decay_log, axis=0)
    inflow = jnp.sqrt(-jnp.expm1(2.0 * decay_log))
    intersection = jnp.dot(in_c, in_b.T, preferred_element_type=jnp.float32)
    causal = jnp.arange(length)[:, None] >= jnp.arange(length)[None, :]
    spread = cumulative[:, None, :] - cumulative[None, :, :]
    fading = jnp.where(causal[:, :, None], jnp.exp(jnp.minimum(spread, 0.0)), 0.0)
    mixing = intersection[:, :, None] * fading * inflow[None, :, :]
    within = jnp.einsum("tsh,shp->thp", mixing, values, precision=HIGHEST)
    tail = jnp.exp(cumulative[-1][None, :] - cumulative) * inflow
    state_here = jnp.einsum(
        "sn,sh,shp->hnp", in_b.astype(jnp.float32), tail, values, precision=HIGHEST
    )
    return (within, state_here, cumulative, values)


def finish_heads(within, carried, cumulative, values, in_c, skip_gain):
    result = within + skip_gain[None, :, None] * values
    if carried is not None:
        outer = jnp.einsum("tn,hnp->thp", in_c.astype(jnp.float32), carried, precision=HIGHEST)
        result = result + jnp.exp(cumulative)[:, :, None] * outer
    return result.reshape(result.shape[0], -1).astype(jnp.bfloat16)


def shards(
    tokens,
    ssm_input,
    in_b,
    in_c,
    decay_log,
    skip_gain,
    out_proj,
    norm_gain,
    routes,
    route_gate,
    w_gate,
    w_up,
    w_down,
):
    n_ctx, n_state, n_expert = (lax.axis_size(a) for a in ("ctx", "state", "expert"))
    ctx_at, state_at, expert_at = (lax.axis_index(a) for a in ("ctx", "state", "expert"))
    length, block = tokens.shape
    count = n_ctx * length
    groups = n_state * n_expert
    half = out_proj.shape[1]
    width = half * n_ctx
    ctx = digits_of("ctx", n_ctx)
    state = digits_of("state", n_state)
    expert = digits_of("expert", n_expert)
    expert_down = expert[::-1]

    heads, top = decay_log.shape[1], routes.shape[1]
    small = jnp.concatenate([decay_log.T, route_gate.T, routes.T.astype(jnp.float32)], axis=0)
    raw = [ssm_input, in_b, in_c, small, tokens]
    jobs = [(i, ctx, ctx, (0, a.shape[1])) for i, a in enumerate(raw)]
    all_ssm, all_b, all_c, all_small, all_tokens = gather(raw, jobs, 0)
    all_decay = all_small[:, :heads].transpose(0, 2, 1)
    all_gate = all_small[:, heads : heads + top].transpose(0, 2, 1)
    all_routes = all_small[:, heads + top :].transpose(0, 2, 1).astype(jnp.int32)

    carried, mixed = None, []
    for c in range(n_ctx):
        within, state_here, cumulative, values = block_terms(
            all_ssm[c], all_b[c], all_c[c], all_decay[c]
        )
        mixed.append(finish_heads(within, carried, cumulative, values, all_c[c], skip_gain))
        if carried is None:
            carried = state_here
        else:
            carried = jnp.exp(cumulative[-1])[:, None, None] * carried + state_here
    all_mixed = jnp.concatenate(mixed, axis=0)

    product = jnp.dot(all_mixed, out_proj, preferred_element_type=jnp.float32).astype(jnp.bfloat16)
    own = (state_at * n_expert + expert_at) * block - ctx_at * half
    held = jnp.logical_and(own >= 0, own < half)
    start = jnp.clip(own, 0, half - block)
    patch = lax.dynamic_slice(product, (0, start), (count, block)).astype(jnp.float32)
    patch = patch + jnp.where(held, all_tokens.reshape(count, block).astype(jnp.float32), 0.0)
    summands = lax.dynamic_update_slice(product, patch.astype(jnp.bfloat16), (0, start))
    rows = count // groups
    dims = state + expert_down
    summands = summands.reshape(tuple(d[2] for d in dims) + (rows, half))
    side = expert[1:]
    orders = [expert + state, expert[:1] + state + side]
    parts = [
        (order, 0, rows, k * (half // 2) + start, size)
        for start, size in halves(half // 2)
        for k, order in enumerate(orders)
    ]
    resid_piece = scatter(summands, dims, parts, 1, jnp.bfloat16)

    whole = ctx + dims
    core = expert[:1]
    orders = [state + ctx + side + core, state + side + ctx + core, side + ctx + state + core]
    cuts = [[(a + start, size) for start, size in halves(n)] for a, n in thirds(half, 128)]
    jobs = [(0, whole, order, cut[k]) for k in range(2) for order, cut in zip(orders, cuts)]
    spread_over = state + expert_down
    jobs.append((1, spread_over, spread_over, (0, block)))
    squares = jnp.sum(resid_piece.astype(jnp.float32) ** 2, axis=1)[None, :]
    jobs.append((2, whole, state + ctx + side + core, (0, rows)))
    resid, gain, squares = gather([resid_piece, norm_gain[None, :], squares], jobs, 2)
    squares = squares.reshape(n_ctx, count)
    gain = gain.reshape(n_ctx, 1, half)
    resid = resid.reshape(n_ctx, count, half)

    scale = lax.rsqrt(jnp.sum(squares, axis=0) / width + norm_epsilon)

    routed = all_routes == expert_at
    chosen = jnp.any(routed, axis=2)
    weight = jnp.sum(jnp.where(routed, all_gate, 0.0), axis=2).reshape(count)
    flags = chosen.astype(jnp.bfloat16)
    earlier = (jnp.arange(length)[:, None] < jnp.arange(length)[None, :]).astype(jnp.bfloat16)
    slot = jnp.dot(flags, earlier, preferred_element_type=jnp.float32).astype(jnp.int32)
    target = jnp.where(chosen, slot + MOST * jnp.arange(n_ctx, dtype=jnp.int32)[:, None], -1)
    hits = jnp.arange(n_ctx * MOST, dtype=jnp.int32)[:, None] == target.reshape(1, count)
    dispatch = hits.astype(jnp.bfloat16)
    slot_weight = jnp.sum(jnp.where(hits, weight[None, :], 0.0), axis=1)
    slot_scale = jnp.sum(jnp.where(hits, scale[None, :], 0.0), axis=1)

    picked = jnp.einsum("rt,ctd->crd", dispatch, resid, preferred_element_type=jnp.float32)
    entering = (picked * slot_scale[None, :, None] * gain).astype(jnp.bfloat16)
    gate_parts = w_gate.reshape(n_ctx, half, w_gate.shape[2])
    up_parts = w_up.reshape(n_ctx, half, w_up.shape[2])
    gate_value = jnp.einsum("crd,cdh->rh", entering, gate_parts, preferred_element_type=jnp.float32)
    up_value = jnp.einsum("crd,cdh->rh", entering, up_parts, preferred_element_type=jnp.float32)
    hidden = (jax.nn.silu(gate_value) * up_value * slot_weight[:, None]).astype(jnp.bfloat16)
    terms = jnp.dot(hidden, w_down[0], preferred_element_type=jnp.float32).astype(jnp.bfloat16)
    spread = jnp.einsum(
        "rt,rgd->gtd", dispatch, terms.reshape(-1, groups, block), preferred_element_type=jnp.float32
    ).astype(jnp.bfloat16)
    dims = state + expert_down + ctx
    spread = spread.reshape(tuple(d[2] for d in dims) + (length, block))
    orders = [core + side + ctx + state, core + ctx + side + state, core + state + side + ctx]
    parts = [
        (order, r0, n, start, size)
        for start, size in halves(block)
        for order, (r0, n) in zip(orders, thirds(length, 16))
    ]
    combined = scatter(spread, dims, parts, 3, jnp.float32)

    position = (state_at * n_expert + expert_at) * block
    own_resid = lax.dynamic_slice(
        resid, (position // half, ctx_at * length, position % half), (1, length, block)
    )[0]
    return (own_resid.astype(jnp.float32) + combined).astype(jnp.bfloat16)


def solution(mesh):
    in_specs = (
        P("ctx", ("state", "expert")),
        P("ctx", ("state", "expert")),
        P("ctx", None),
        P("ctx", None),
        P("ctx", ("state", "expert")),
        P(("state", "expert")),
        P(("state", "expert"), "ctx"),
        P(("state", "expert")),
        P("ctx", None),
        P("ctx", None),
        P("expert", None, ("ctx", "state")),
        P("expert", None, ("ctx", "state")),
        P("expert", ("ctx", "state"), None),
    )
    out_specs = P("ctx", ("state", "expert"))
    return jax.shard_map(shards, mesh=mesh, in_specs=in_specs, out_specs=out_specs, check_vma=False)
```
